32 devices in a mesh: band: 4 (over y, x), query: 8 (over z, core).
Axes of the slice: x: 2, y: 2, z: 4, core: 2. Of those that a mesh axis runs over, the one named last changes fastest.
Arguments:
- spectra: bfloat16 [192, 20480], P('band'), may hold values from 0 to 3
- theo: bfloat16 [8, 8, 20480], P('query', 'band'), may hold values from -0.0390625 to 0.0390625
- offsets: int32 [16], replicated, may hold values from -128 to 128
- win_lo: int32 [192], P('band'), may hold values from 0 to 32
- win_len: int32 [192], P('band'), may hold values from 1 to 32
Outputs:
- best: float32 [192, 16], P(('band', 'query'))
- average: float32 [192, 16], P(('band', 'query'))
The draws below stay inside these ranges and needn't reach their ends.
Inputs may be any that keep to these rules, and one draw needn't show every extreme that they name: win_lo + win_len never exceeds 64.
All inputs are finite; a program needn't handle non-finite values.
Results may differ from the reference program's by a relative error of at most 0.003.
Values may be sent and summed in bfloat16 or wider, within the bound.
A program may use at most 128 MiB of HBM per device.

```python
import jax
import jax.numpy as jnp
from jax import lax

BINS = 20480
SHIFTS = 16
BG_HALF = 75
SHIFT_MAX = 128
GP = 8
PEPS = 64
SPECTRA = 192
WIN_MAX = 32
N_QUERY = 8


def place_ends(values, stream_key, smallest, largest):
    longest = values.shape.index(max(values.shape))
    spots = []
    for shift in (0, 1):
        where = [jax.random.randint(jax.random.fold_in(stream_key, axis), (), 0, length) for axis, length in enumerate(values.shape)]
        where[longest] = (where[longest] + shift) % values.shape[longest]
        spots.append(tuple(where))
    return values.at[spots[0]].set(smallest).at[spots[1]].set(largest)


def steps_of(key, shape, pieces, smallest, largest):
    gain = 1.0
    for position, shards_of in pieces:
        draws = jax.random.uniform(jax.random.fold_in(jax.random.fold_in(key, 6), position), (shards_of,), jnp.float32, smallest / len(pieces), largest / len(pieces))
        gain = gain * jnp.repeat(jnp.exp(draws), shape[position] // shards_of).reshape((-1,) + (1,) * (len(shape) - 1 - position))
    return gain


def gaussian(key, extent, scale, bound, split=(), kind=jnp.bfloat16):
    level = steps_of(key, extent, split, -0.22, 0.18) if split else 1.0
    result = jax.random.normal(key, extent, jnp.float32) * scale * level
    return jnp.minimum(jnp.maximum(result, -bound), bound).astype(kind)


def setup_inputs(seed: int = 0) -> dict:
    streams_of = jax.random.split(jax.random.key(seed), 6)
    return {
        "spectra": jnp.clip(3.0 * jax.random.uniform(streams_of[0], (SPECTRA, BINS), jnp.float32) ** steps_of(streams_of[0], (SPECTRA, BINS), ((0, 4),), -0.2, 0.2), 0.0, 3.0).astype(jnp.bfloat16),
        "theo": gaussian(streams_of[1], (N_QUERY, GP, BINS), BINS ** -0.5, 0.0390625, ((0, 8), (1, 4))),
        "offsets": place_ends(jax.random.randint(streams_of[2], (SHIFTS,), 0 - SHIFT_MAX, SHIFT_MAX + 1), jax.random.fold_in(streams_of[2], 1), 0 - SHIFT_MAX, SHIFT_MAX).astype(jnp.int32),
        "win_lo": place_ends(jax.random.randint(streams_of[3], (SPECTRA,), 0, PEPS - WIN_MAX + 1), jax.random.fold_in(streams_of[3], 1), 0, PEPS - WIN_MAX).astype(jnp.int32),
        "win_len": place_ends(jax.random.randint(streams_of[4], (SPECTRA,), 1, WIN_MAX + 1), jax.random.fold_in(streams_of[4], 1), 1, WIN_MAX).astype(jnp.int32),
    }


def reference(spectra, theo, offsets, win_lo, win_len):
    intensity = spectra.astype(jnp.float32)
    padded = jnp.pad(intensity, ((0, 0), (BG_HALF, BG_HALF)))
    window_sum = lax.reduce_window(padded, jnp.float32(0.0), lax.add, (1, 2 * BG_HALF + 1), (1, 1), "VALID")
    box_sum = window_sum - intensity
    corrected = (intensity - box_sum / (2.0 * BG_HALF)).astype(jnp.bfloat16)
    corrected_pad = jnp.pad(corrected.astype(jnp.float32), ((0, 0), (SHIFT_MAX, SHIFT_MAX)))
    peptide_rows = theo.reshape(PEPS, BINS).astype(jnp.float32)

    def one_shift(offset):
        shifted = lax.dynamic_slice_in_dim(corrected_pad, (SHIFT_MAX + offset).astype(jnp.int32), BINS, 1)
        return jnp.dot(shifted, peptide_rows.T, preferred_element_type=jnp.float32, precision=lax.Precision.HIGHEST)

    scores = lax.map(one_shift, offsets)
    peptide_index = jnp.arange(PEPS, dtype=jnp.int32)
    inside = (peptide_index[None, :] >= win_lo[:, None]) & (peptide_index[None, :] < (win_lo + win_len)[:, None])
    best_score = jnp.max(jnp.where(inside[None], scores, -jnp.inf), axis=2).T
    totals = jnp.sum(jnp.where(inside[None], scores, jnp.float32(0.0)), axis=2).T
    average = totals / win_len[:, None].astype(jnp.float32)
    return best_score, average
```

```python
import functools

import jax
import jax.numpy as jnp
from jax import lax
from jax.experimental import pallas as pl
from jax.experimental.pallas import tpu as pltpu
from jax.sharding import PartitionSpec as P

BG_HALF = 75
SHIFT_MAX = 128
LANES = 128
BLOCK = 256
BOX_BLOCKS = 8
STEP = 512
MESH = pl.DeviceIdType.MESH


def box_tables():
    row = lax.broadcasted_iota(jnp.int32, (BLOCK, BLOCK), 0)
    target = lax.broadcasted_iota(jnp.int32, (BLOCK, BLOCK), 1)
    gap = row - target
    middle = (jnp.abs(gap) <= BG_HALF) & (gap != 0)
    side_gap = jnp.where(row < LANES, row - LANES, row + LANES) - target
    side = jnp.abs(side_gap) <= BG_HALF
    return middle.astype(jnp.float32).astype(jnp.bfloat16), side.astype(jnp.float32).astype(jnp.bfloat16)


def column(values, rows):
    row = lax.broadcasted_iota(jnp.int32, (rows, rows), 0)
    lane = lax.broadcasted_iota(jnp.int32, (rows, rows), 1)
    spread = jnp.broadcast_to(values.astype(jnp.float32).reshape(1, rows), (rows, rows))
    return jnp.sum(jnp.where(row == lane, spread, 0.0), axis=1, keepdims=True)


def kernel(
    nb, nq,
    spectra_ref, theo_ref, offsets_ref, lo_ref, len_ref,
    best_ref, average_ref,
    spec, corr, gathered, theo32, tables, send, recv,
    spec_sem, own_sem, band_send, band_recv, query_send, query_recv,
):
    rows, bins = spectra_ref.shape
    peps = theo_ref.shape[1]
    shifts = offsets_ref.shape[0]
    own = rows // nq
    blocks = bins // LANES
    per_chunk = 8 // peps
    chunks = nb * peps // 8
    width = BLOCK * BOX_BLOCKS
    box_steps = bins // width
    band = lax.axis_index("band")
    query = lax.axis_index("query")

    def spec_copy(i):
        start = pl.multiple_of(i * width, width)
        return pltpu.make_async_copy(
            spectra_ref.at[:, pl.ds(start, width)],
            spec.at[:, pl.ds(pl.multiple_of(start + LANES, LANES), width)],
            spec_sem.at[i],
        )

    for i in range(box_steps):
        spec_copy(i).start()
    own_copy = pltpu.make_async_copy(theo_ref.at[0], gathered.at[0], own_sem)
    own_copy.start()

    barrier = pltpu.get_barrier_semaphore()
    for d in range(1, nb):
        pl.semaphore_signal(barrier, inc=1, device_id={"band": lax.rem(band + d, nb)}, device_id_type=MESH)
    for d in range(1, nq):
        pl.semaphore_signal(barrier, inc=1, device_id={"query": lax.rem(query + d, nq)}, device_id_type=MESH)
    pl.semaphore_wait(barrier, nb - 1 + nq - 1)

    def theo_copy(d):
        return pltpu.make_async_remote_copy(
            src_ref=theo_ref.at[0],
            dst_ref=gathered.at[d],
            send_sem=band_send.at[d],
            recv_sem=band_recv.at[d],
            device_id={"band": lax.rem(band + d, nb)},
            device_id_type=MESH,
        )

    for d in range(1, nb):
        theo_copy(d).start()

    spec[:, :LANES] = jnp.zeros((rows, LANES), spec.dtype)
    spec[:, LANES + bins:] = jnp.zeros((rows, LANES), spec.dtype)
    tables[0], tables[1] = box_tables()
    send[...] = jnp.zeros_like(send)
    zero_block = jnp.zeros((8, LANES), jnp.float32)
    for c in range(chunks):
        theo32[c, 0] = zero_block
        theo32[c, blocks + 1] = zero_block
        theo32[c, blocks + 2] = zero_block
    lo = column(lo_ref[...], rows)
    length = column(len_ref[...], rows)
    high = lo + length

    spec_copy(0).wait()

    @pl.loop(0, box_steps)
    def _(i):
        @pl.when(i + 1 < box_steps)
        def _():
            spec_copy(i + 1).wait()

        start = pl.multiple_of(i * width, width)
        middles, sides = [], []
        for j in range(BOX_BLOCKS):
            at = start + j * BLOCK
            before = spec[:, pl.ds(pl.multiple_of(at, LANES), LANES)]
            middles.append(spec[:, pl.ds(pl.multiple_of(at + LANES, LANES), BLOCK)])
            after = spec[:, pl.ds(pl.multiple_of(at + LANES + BLOCK, LANES), LANES)]
            sides.append(jnp.concatenate([before, after], axis=1))
        box = jnp.dot(jnp.concatenate(middles, axis=0), tables[0], preferred_element_type=jnp.float32)
        box += jnp.dot(jnp.concatenate(sides, axis=0), tables[1], preferred_element_type=jnp.float32)
        for j in range(BOX_BLOCKS):
            level = box[j * rows:(j + 1) * rows] * (1.0 / (2.0 * BG_HALF))
            fixed = middles[j].astype(jnp.float32) - level
            corr[:, pl.ds(pl.multiple_of(start + j * BLOCK, BLOCK), BLOCK)] = fixed.astype(jnp.bfloat16)

    own_copy.wait()
    for d in range(1, nb):
        theo_copy(d).wait_recv()

    for c in range(chunks):
        @pl.loop(0, blocks, unroll=4)
        def _(b):
            at = pl.ds(pl.multiple_of(b * LANES, LANES), LANES)
            parts = []
            for j in range(per_chunk):
                slot = lax.rem(band - (c * per_chunk + j) + nb, nb)
                parts.append(gathered[slot, :, at].astype(jnp.float32))
            theo32[c, b + 1] = jnp.concatenate(parts, axis=0)

    lane = lax.broadcasted_iota(jnp.int32, (8, LANES), 1)
    ahead = [SHIFT_MAX - offsets_ref[k] for k in range(shifts)]
    skip = [a // LANES for a in ahead]
    rest = [a % LANES for a in ahead]
    turn = [(LANES - r) % LANES for r in rest]

    wide = shifts * 8
    peptide = lax.broadcasted_iota(jnp.int32, (rows, wide), 1) % 8
    best = jnp.full((rows, wide), -jnp.inf, jnp.float32)
    total = jnp.zeros((rows, wide), jnp.float32)
    for c in range(chunks):
        def step(i, acc):
            first = i * (STEP // LANES)
            columns = []
            for j in range(STEP // LANES):
                parts = []
                for k in range(shifts):
                    near = theo32[c, first + j + skip[k]]
                    far = theo32[c, first + j + skip[k] + 1]
                    parts.append(pltpu.roll(jnp.where(lane < rest[k], far, near), turn[k], 1))
                columns.append(jnp.concatenate(parts, axis=0).astype(jnp.bfloat16))
            shifted = jnp.concatenate(columns, axis=1)
            piece = corr[:, pl.ds(pl.multiple_of(i * STEP, STEP), STEP)]
            return acc + lax.dot_general(
                piece, shifted, (((1,), (1,)), ((), ())), preferred_element_type=jnp.float32
            )

        scores = lax.fori_loop(0, bins // STEP, step, jnp.zeros((rows, wide), jnp.float32))
        number = (peptide + (query * (chunks * 8) + c * 8)).astype(jnp.float32)
        inside = (number >= lo) & (number < high)
        best = jnp.maximum(best, jnp.where(inside, scores, -jnp.inf))
        total = total + jnp.where(inside, scores, 0.0)

    for reach in (4, 2, 1):
        best = jnp.maximum(best, pltpu.roll(best, wide - reach, 1))
        total = total + pltpu.roll(total, wide - reach, 1)
    total = total / length
    spread = lax.broadcasted_iota(jnp.int32, (rows, wide), 1)
    pick = (spread % shifts) * 8
    best = jnp.take_along_axis(best, pick, axis=1)
    total = jnp.take_along_axis(total, pick, axis=1)
    packed = jnp.where(spread < shifts, best, total)
    for q in range(nq):
        send[q, :own] = packed[q * own:(q + 1) * own]

    def result_copy(d):
        return pltpu.make_async_remote_copy(
            src_ref=send.at[lax.rem(query + d, nq)],
            dst_ref=recv.at[d],
            send_sem=query_send.at[d],
            recv_sem=query_recv.at[d],
            device_id={"query": lax.rem(query + d, nq)},
            device_id_type=MESH,
        )

    for d in range(1, nq):
        result_copy(d).start()
    mine = send[query]
    top, mean = mine, mine
    for d in range(1, nq):
        result_copy(d).wait_recv()
        top = jnp.maximum(top, recv[d])
        mean = mean + recv[d]
    best_ref[...] = top[:own, :shifts]
    average_ref[...] = mean[:own, shifts:2 * shifts]
    for d in range(1, nb):
        theo_copy(d).wait_send()
    for d in range(1, nq):
        result_copy(d).wait_send()


def local(spectra, theo, offsets, win_lo, win_len):
    nb, nq = lax.axis_size("band"), lax.axis_size("query")
    rows, bins = spectra.shape
    peps = theo.shape[1]
    shifts = offsets.shape[0]
    own = rows // nq
    slots = (own + 7) // 8 * 8
    chunks = nb * peps // 8
    result = jax.ShapeDtypeStruct((own, shifts), jnp.float32)
    vmem = pl.BlockSpec(memory_space=pltpu.VMEM)
    return pl.pallas_call(
        functools.partial(kernel, nb, nq),
        out_shape=(result, result),
        in_specs=[
            pl.BlockSpec(memory_space=pl.ANY),
            pl.BlockSpec(memory_space=pl.ANY),
            pl.BlockSpec(memory_space=pltpu.SMEM),
            vmem,
            vmem,
        ],
        out_specs=(vmem, vmem),
        scratch_shapes=[
            pltpu.VMEM((rows, bins + 2 * LANES), jnp.bfloat16),
            pltpu.VMEM((rows, bins), jnp.bfloat16),
            pltpu.VMEM((nb, peps, bins), jnp.bfloat16),
            pltpu.VMEM((chunks, bins // LANES + 3, 8, LANES), jnp.float32),
            pltpu.VMEM((2, BLOCK, BLOCK), jnp.bfloat16),
            pltpu.VMEM((nq, slots, LANES), jnp.float32),
            pltpu.VMEM((nq, slots, LANES), jnp.float32),
            pltpu.SemaphoreType.DMA((bins // (BLOCK * BOX_BLOCKS),)),
            pltpu.SemaphoreType.DMA,
            pltpu.SemaphoreType.DMA((nb,)),
            pltpu.SemaphoreType.DMA((nb,)),
            pltpu.SemaphoreType.DMA((nq,)),
            pltpu.SemaphoreType.DMA((nq,)),
        ],
        compiler_params=pltpu.CompilerParams(
            collective_id=0, has_side_effects=True, vmem_limit_bytes=48 * 2**20
        ),
        name="shifted_scores",
    )(spectra, theo, offsets, win_lo, win_len)


def solution(mesh):
    placed = (P("band", None), P("query", "band", None), P(), P("band"), P("band"))
    return jax.shard_map(
        local,
        mesh=mesh,
        in_specs=placed,
        out_specs=(P(("band", "query"), None), P(("band", "query"), None)),
        check_vma=False,
    )
```

```python
import functools

import jax
import jax.numpy as jnp
from jax import lax
from jax.experimental import pallas as pl
from jax.experimental.pallas import tpu as pltpu
from jax.sharding import PartitionSpec as P

BG_HALF = 75
SHIFT_MAX = 128
LANES = 128
BLOCK = 256
BOX_BLOCKS = 8
STEP = 2048
MESH = pl.DeviceIdType.MESH


def box_tables():
    row = lax.broadcasted_iota(jnp.int32, (BLOCK, BLOCK), 0)
    target = lax.broadcasted_iota(jnp.int32, (BLOCK, BLOCK), 1)
    gap = row - target
    middle = (jnp.abs(gap) <= BG_HALF) & (gap != 0)
    side_gap = jnp.where(row < LANES, row - LANES, row + LANES) - target
    side = jnp.abs(side_gap) <= BG_HALF
    return middle.astype(jnp.float32).astype(jnp.bfloat16), side.astype(jnp.float32).astype(jnp.bfloat16)


def column(values, rows):
    row = lax.broadcasted_iota(jnp.int32, (rows, rows), 0)
    lane = lax.broadcasted_iota(jnp.int32, (rows, rows), 1)
    spread = jnp.broadcast_to(values.astype(jnp.float32).reshape(1, rows), (rows, rows))
    return jnp.sum(jnp.where(row == lane, spread, 0.0), axis=1, keepdims=True)


def kernel(
    nb, nq,
    spectra_ref, theo_ref, offsets_hbm, lo_hbm, len_hbm,
    best_ref, average_ref,
    spec, corr, gathered, theo32, tables, send, recv,
    offsets_ref, lo_ref, len_ref, small_sem, spec_sem, own_sem, band_send, band_recv, query_send, query_recv,
):
    rows, bins = spectra_ref.shape
    peps = theo_ref.shape[1]
    shifts = offsets_hbm.shape[0]
    own = rows // nq
    blocks = bins // LANES
    per_chunk = 8 // peps
    chunks = nb * peps // 8
    width = BLOCK * BOX_BLOCKS
    box_steps = bins // width
    band = lax.axis_index("band")
    query = lax.axis_index("query")

    def spec_copy(i):
        start = pl.multiple_of(i * width, width)
        return pltpu.make_async_copy(
            spectra_ref.at[:, pl.ds(start, width)],
            spec.at[:, pl.ds(pl.multiple_of(start + LANES, LANES), width)],
            spec_sem.at[i],
        )

    for i in range(box_steps):
        spec_copy(i).start()
    own_copy = pltpu.make_async_copy(theo_ref.at[0], gathered.at[0], own_sem)
    own_copy.start()
    small = [
        pltpu.make_async_copy(source, target, small_sem.at[i])
        for i, (source, target) in enumerate(
            [(offsets_hbm, offsets_ref), (lo_hbm, lo_ref), (len_hbm, len_ref)]
        )
    ]
    for copy in small:
        copy.start()

    barrier = pltpu.get_barrier_semaphore()
    for d in range(1, nb):
        pl.semaphore_signal(barrier, inc=1, device_id={"band": lax.rem(band + d, nb)}, device_id_type=MESH)
    for d in range(1, nq):
        pl.semaphore_signal(barrier, inc=1, device_id={"query": lax.rem(query + d, nq)}, device_id_type=MESH)
    pl.semaphore_wait(barrier, nb - 1 + nq - 1)

    def theo_copy(d):
        return pltpu.make_async_remote_copy(
            src_ref=theo_ref.at[0],
            dst_ref=gathered.at[d],
            send_sem=band_send.at[d],
            recv_sem=band_recv.at[d],
            device_id={"band": lax.rem(band + d, nb)},
            device_id_type=MESH,
        )

    for d in range(1, nb):
        theo_copy(d).start()

    spec[:, :LANES] = jnp.zeros((rows, LANES), spec.dtype)
    spec[:, LANES + bins:] = jnp.zeros((rows, LANES), spec.dtype)
    tables[0], tables[1] = box_tables()
    send[...] = jnp.zeros_like(send)
    zero_block = jnp.zeros((8, LANES), jnp.float32)
    for c in range(chunks):
        theo32[c, 0] = zero_block
        theo32[c, blocks + 1] = zero_block
        theo32[c, blocks + 2] = zero_block
    for copy in small:
        copy.wait()
    lo = column(lo_ref[...], rows)
    length = column(len_ref[...], rows)
    high = lo + length

    spec_copy(0).wait()

    @pl.loop(0, box_steps)
    def _(i):
        @pl.when(i + 1 < box_steps)
        def _():
            spec_copy(i + 1).wait()

        start = pl.multiple_of(i * width, width)
        middles, sides = [], []
        for j in range(BOX_BLOCKS):
            at = start + j * BLOCK
            before = spec[:, pl.ds(pl.multiple_of(at, LANES), LANES)]
            middles.append(spec[:, pl.ds(pl.multiple_of(at + LANES, LANES), BLOCK)])
            after = spec[:, pl.ds(pl.multiple_of(at + LANES + BLOCK, LANES), LANES)]
            sides.append(jnp.concatenate([before, after], axis=1))
        box = jnp.dot(jnp.concatenate(middles, axis=0), tables[0], preferred_element_type=jnp.float32)
        box += jnp.dot(jnp.concatenate(sides, axis=0), tables[1], preferred_element_type=jnp.float32)
        for j in range(BOX_BLOCKS):
            level = box[j * rows:(j + 1) * rows] * (1.0 / (2.0 * BG_HALF))
            fixed = middles[j].astype(jnp.float32) - level
            corr[:, pl.ds(pl.multiple_of(start + j * BLOCK, BLOCK), BLOCK)] = fixed.astype(jnp.bfloat16)

    own_copy.wait()
    for d in range(1, nb):
        theo_copy(d).wait_recv()

    for c in range(chunks):
        @pl.loop(0, blocks, unroll=4)
        def _(b):
            at = pl.ds(pl.multiple_of(b * LANES, LANES), LANES)
            parts = []
            for j in range(per_chunk):
                slot = lax.rem(band - (c * per_chunk + j) + nb, nb)
                parts.append(gathered[slot, :, at].astype(jnp.float32))
            theo32[c, b + 1] = jnp.concatenate(parts, axis=0)

    lane = lax.broadcasted_iota(jnp.int32, (8, LANES), 1)
    ahead = [SHIFT_MAX - offsets_ref[k] for k in range(shifts)]
    skip = [a // LANES for a in ahead]
    rest = [a % LANES for a in ahead]
    turn = [(LANES - r) % LANES for r in rest]

    wide = shifts * 8
    peptide = lax.broadcasted_iota(jnp.int32, (rows, wide), 1) % 8
    best = jnp.full((rows, wide), -jnp.inf, jnp.float32)
    total = jnp.zeros((rows, wide), jnp.float32)
    for c in range(chunks):
        def step(i, acc):
            first = i * (STEP // LANES)
            columns = []
            for j in range(STEP // LANES):
                parts = []
                for k in range(shifts):
                    near = theo32[c, first + j + skip[k]]
                    far = theo32[c, first + j + skip[k] + 1]
                    parts.append(pltpu.roll(jnp.where(lane < rest[k], far, near), turn[k], 1))
                columns.append(jnp.concatenate(parts, axis=0).astype(jnp.bfloat16))
            shifted = jnp.concatenate(columns, axis=1)
            piece = corr[:, pl.ds(pl.multiple_of(i * STEP, STEP), STEP)]
            return acc + lax.dot_general(
                piece, shifted, (((1,), (1,)), ((), ())), preferred_element_type=jnp.float32
            )

        scores = lax.fori_loop(0, bins // STEP, step, jnp.zeros((rows, wide), jnp.float32))
        number = (peptide + (query * (chunks * 8) + c * 8)).astype(jnp.float32)
        inside = (number >= lo) & (number < high)
        best = jnp.maximum(best, jnp.where(inside, scores, -jnp.inf))
        total = total + jnp.where(inside, scores, 0.0)

    for reach in (4, 2, 1):
        best = jnp.maximum(best, pltpu.roll(best, wide - reach, 1))
        total = total + pltpu.roll(total, wide - reach, 1)
    total = total / length
    spread = lax.broadcasted_iota(jnp.int32, (rows, wide), 1)
    pick = (spread % shifts) * 8
    best = jnp.take_along_axis(best, pick, axis=1)
    total = jnp.take_along_axis(total, pick, axis=1)
    packed = jnp.where(spread < shifts, best, total)
    for q in range(nq):
        send[q, :own] = packed[q * own:(q + 1) * own]

    def result_copy(d):
        return pltpu.make_async_remote_copy(
            src_ref=send.at[lax.rem(query + d, nq)],
            dst_ref=recv.at[d],
            send_sem=query_send.at[d],
            recv_sem=query_recv.at[d],
            device_id={"query": lax.rem(query + d, nq)},
            device_id_type=MESH,
        )

    for d in range(1, nq):
        result_copy(d).start()
    mine = send[query]
    top, mean = mine, mine
    for d in range(1, nq):
        result_copy(d).wait_recv()
        top = jnp.maximum(top, recv[d])
        mean = mean + recv[d]
    best_ref[...] = top[:own, :shifts]
    average_ref[...] = mean[:own, shifts:2 * shifts]
    for d in range(1, nb):
        theo_copy(d).wait_send()
    for d in range(1, nq):
        result_copy(d).wait_send()


def local(spectra, theo, offsets, win_lo, win_len):
    nb, nq = lax.axis_size("band"), lax.axis_size("query")
    rows, bins = spectra.shape
    peps = theo.shape[1]
    shifts = offsets.shape[0]
    own = rows // nq
    slots = (own + 7) // 8 * 8
    chunks = nb * peps // 8
    result = jax.ShapeDtypeStruct((own, shifts), jnp.float32)
    vmem = pl.BlockSpec(memory_space=pltpu.VMEM)
    return pl.pallas_call(
        functools.partial(kernel, nb, nq),
        out_shape=(result, result),
        in_specs=[
            pl.BlockSpec(memory_space=pltpu.HBM),
        ] * 5,
        out_specs=(vmem, vmem),
        scratch_shapes=[
            pltpu.VMEM((rows, bins + 2 * LANES), jnp.bfloat16),
            pltpu.VMEM((rows, bins), jnp.bfloat16),
            pltpu.VMEM((nb, peps, bins), jnp.bfloat16),
            pltpu.VMEM((chunks, bins // LANES + 3, 8, LANES), jnp.float32),
            pltpu.VMEM((2, BLOCK, BLOCK), jnp.bfloat16),
            pltpu.VMEM((nq, slots, LANES), jnp.float32),
            pltpu.VMEM((nq, slots, LANES), jnp.float32),
            pltpu.SMEM((shifts,), jnp.int32),
            pltpu.VMEM((rows,), jnp.int32),
            pltpu.VMEM((rows,), jnp.int32),
            pltpu.SemaphoreType.DMA((3,)),
            pltpu.SemaphoreType.DMA((bins // (BLOCK * BOX_BLOCKS),)),
            pltpu.SemaphoreType.DMA,
            pltpu.SemaphoreType.DMA((nb,)),
            pltpu.SemaphoreType.DMA((nb,)),
            pltpu.SemaphoreType.DMA((nq,)),
            pltpu.SemaphoreType.DMA((nq,)),
        ],
        compiler_params=pltpu.CompilerParams(
            collective_id=0, has_side_effects=True, vmem_limit_bytes=64 * 2**20
        ),
        name="shifted_scores",
    )(spectra, theo, offsets, win_lo, win_len)


def solution(mesh):
    placed = (P("band", None), P("query", "band", None), P(), P("band"), P("band"))
    return jax.shard_map(
        local,
        mesh=mesh,
        in_specs=placed,
        out_specs=(P(("band", "query"), None), P(("band", "query"), None)),
        check_vma=False,
    )
```

```python
import functools

import jax
import jax.numpy as jnp
from jax import lax
from jax.experimental import pallas as pl
from jax.experimental.pallas import tpu as pltpu
from jax.sharding import PartitionSpec as P

BG_HALF = 75
SHIFT_MAX = 128
LANES = 128
BLOCK = 256
BOX_BLOCKS = 8
STEP = 2048
PARTS = 2
MESH = pl.DeviceIdType.MESH


def box_tables():
    row = lax.broadcasted_iota(jnp.int32, (BLOCK, BLOCK), 0)
    target = lax.broadcasted_iota(jnp.int32, (BLOCK, BLOCK), 1)
    gap = row - target
    middle = (jnp.abs(gap) <= BG_HALF) & (gap != 0)
    side_gap = jnp.where(row < LANES, row - LANES, row + LANES) - target
    side = jnp.abs(side_gap) <= BG_HALF
    return middle.astype(jnp.float32).astype(jnp.bfloat16), side.astype(jnp.float32).astype(jnp.bfloat16)


def column(values, rows):
    row = lax.broadcasted_iota(jnp.int32, (rows, rows), 0)
    lane = lax.broadcasted_iota(jnp.int32, (rows, rows), 1)
    spread = jnp.broadcast_to(values.astype(jnp.float32).reshape(1, rows), (rows, rows))
    return jnp.sum(jnp.where(row == lane, spread, 0.0), axis=1, keepdims=True)


def kernel(
    nb, nq,
    spectra_ref, theo_ref, offsets_hbm, lo_hbm, len_hbm,
    out_ref,
    spec, corr, gathered, pairs, tables, send, recv,
    offsets_ref, lo_ref, len_ref, small_sem, spec_sem, own_sem, band_send, band_recv, query_send, query_recv,
):
    rows, bins = spectra_ref.shape
    peps = theo_ref.shape[1]
    shifts = offsets_hbm.shape[0]
    own = rows // nq
    blocks = bins // LANES
    per_chunk = 8 // peps
    chunks = nb * peps // 8
    width = BLOCK * BOX_BLOCKS
    box_steps = bins // width
    band = lax.axis_index("band")
    query = lax.axis_index("query")

    def spec_copy(i):
        start = pl.multiple_of(i * width, width)
        return pltpu.make_async_copy(
            spectra_ref.at[:, pl.ds(start, width)],
            spec.at[:, pl.ds(pl.multiple_of(start + LANES, LANES), width)],
            spec_sem.at[i],
        )

    for i in range(box_steps):
        spec_copy(i).start()
    own_copy = pltpu.make_async_copy(theo_ref.at[0], gathered.at[0, :, pl.ds(0, bins)], own_sem)
    own_copy.start()
    small = [
        pltpu.make_async_copy(source, target, small_sem.at[i])
        for i, (source, target) in enumerate(
            [(offsets_hbm, offsets_ref), (lo_hbm, lo_ref), (len_hbm, len_ref)]
        )
    ]
    for copy in small:
        copy.start()

    barrier = pltpu.get_barrier_semaphore()
    for d in range(1, nb):
        pl.semaphore_signal(barrier, inc=1, device_id={"band": lax.rem(band + d, nb)}, device_id_type=MESH)
    for d in range(1, nq):
        pl.semaphore_signal(barrier, inc=1, device_id={"query": lax.rem(query + d, nq)}, device_id_type=MESH)
    pl.semaphore_wait(barrier, nb - 1 + nq - 1)

    part = bins // PARTS

    def theo_copy(d, h):
        return pltpu.make_async_remote_copy(
            src_ref=theo_ref.at[0, :, pl.ds(h * part, part)],
            dst_ref=gathered.at[d, :, pl.ds(h * part, part)],
            send_sem=band_send.at[d, h],
            recv_sem=band_recv.at[d, h],
            device_id={"band": lax.rem(band + d, nb)},
            device_id_type=MESH,
        )

    for h in range(PARTS):
        for d in range(1, nb):
            theo_copy(d, h).start()

    spec[:, :LANES] = jnp.zeros((rows, LANES), spec.dtype)
    spec[:, LANES + bins:] = jnp.zeros((rows, LANES), spec.dtype)
    tables[0], tables[1] = box_tables()
    send[...] = jnp.zeros_like(send)
    gathered[:, :, bins:] = jnp.zeros((nb, peps, LANES), gathered.dtype)
    for c in range(chunks):
        pairs[c, blocks + 1] = jnp.zeros((16, LANES), pairs.dtype)
    for copy in small:
        copy.wait()
    lo = column(lo_ref[...], rows)
    length = column(len_ref[...], rows)
    high = lo + length

    spec_copy(0).wait()

    @pl.loop(0, box_steps)
    def _(i):
        @pl.when(i + 1 < box_steps)
        def _():
            spec_copy(i + 1).wait()

        start = pl.multiple_of(i * width, width)
        middles, sides = [], []
        for j in range(BOX_BLOCKS):
            at = start + j * BLOCK
            before = spec[:, pl.ds(pl.multiple_of(at, LANES), LANES)]
            middles.append(spec[:, pl.ds(pl.multiple_of(at + LANES, LANES), BLOCK)])
            after = spec[:, pl.ds(pl.multiple_of(at + LANES + BLOCK, LANES), LANES)]
            sides.append(jnp.concatenate([before, after], axis=1))
        box = jnp.dot(jnp.concatenate(middles, axis=0), tables[0], preferred_element_type=jnp.float32)
        box += jnp.dot(jnp.concatenate(sides, axis=0), tables[1], preferred_element_type=jnp.float32)
        for j in range(BOX_BLOCKS):
            level = box[j * rows:(j + 1) * rows] * (1.0 / (2.0 * BG_HALF))
            fixed = middles[j].astype(jnp.float32) - level
            corr[:, pl.ds(pl.multiple_of(start + j * BLOCK, BLOCK), BLOCK)] = fixed.astype(jnp.bfloat16)

    own_copy.wait()
    lane = lax.broadcasted_iota(jnp.int32, (16, LANES), 1).astype(jnp.float32).astype(jnp.bfloat16)
    ahead = [SHIFT_MAX - offsets_ref[k] for k in range(shifts)]
    skip = [a // LANES for a in ahead]
    rest = [a % LANES for a in ahead]
    turn = [(LANES - r) % LANES for r in rest]
    edge = [jnp.full((16, LANES), r.astype(jnp.float32)).astype(jnp.bfloat16) for r in rest]
    per_step = STEP // LANES
    wide = shifts * 16

    def read_blocks(c, first):
        at = pl.ds(pl.multiple_of(first * LANES, LANES), 9 * LANES)
        rows_of = []
        for j in range(per_chunk):
            slot = lax.rem(band - (c * per_chunk + j) + nb, nb)
            rows_of.append(gathered[slot, :, at].astype(jnp.float32))
        whole = jnp.concatenate(rows_of, axis=0)
        return [whole[:, t * LANES:(t + 1) * LANES] for t in range(9)]

    def pair(c, g):
        found = read_blocks(c, g * 8)
        for t in range(8):
            pairs[c, g * 8 + t + 1] = jnp.concatenate(found[t:t + 2], axis=0).astype(jnp.bfloat16)

    def step(c, i, acc):
        first = i * per_step
        columns, evens, odds = [], [], []
        for j in range(0, per_step, 2):
            parts = []
            for k in range(shifts):
                near = pairs[c, first + j + skip[k]]
                far = pairs[c, first + j + skip[k] + 1]
                parts.append(pltpu.roll(jnp.where(lane < edge[k], far, near), turn[k], 1))
            columns.append(jnp.concatenate(parts, axis=0))
            at = (first + j) * LANES
            evens.append(corr[:, pl.ds(pl.multiple_of(at, LANES), LANES)])
            odds.append(corr[:, pl.ds(pl.multiple_of(at + LANES, LANES), LANES)])
        shifted = jnp.concatenate(columns, axis=1)
        piece = jnp.concatenate(
            [jnp.concatenate(evens, axis=1), jnp.concatenate(odds, axis=1)], axis=0
        )
        return acc + lax.dot_general(
            piece, shifted, (((1,), (1,)), ((), ())), preferred_element_type=jnp.float32
        )

    sums = [jnp.zeros((2 * rows, wide), jnp.float32)] * chunks
    group_from = step_from = 0
    for h in range(PARTS):
        for d in range(1, nb):
            theo_copy(d, h).wait_recv()
        if h < PARTS - 1:
            group_to = ((h + 1) * part // LANES - 1) // 8
            step_to = (group_to * 8 - per_step - 1) // per_step + 1
        else:
            group_to, step_to = blocks // 8, bins // STEP
        for c in range(chunks):
            if h == 0:
                start = read_blocks(c, 0)[0]
                pairs[c, 0] = jnp.concatenate([jnp.zeros_like(start), start], axis=0).astype(jnp.bfloat16)
            pl.loop(group_from, group_to)(functools.partial(pair, c))
            sums[c] = lax.fori_loop(step_from, step_to, functools.partial(step, c), sums[c])
        group_from, step_from = group_to, step_to

    spread = lax.broadcasted_iota(jnp.int32, (rows, wide), 1)
    peptide = spread % 16
    best = jnp.full((rows, wide), -jnp.inf, jnp.float32)
    total = jnp.zeros((rows, wide), jnp.float32)
    for c in range(chunks):
        scores = sums[c][:rows] + pltpu.roll(sums[c][rows:], wide - 8, 1)
        number = (peptide + (query * (chunks * 8) + c * 8)).astype(jnp.float32)
        inside = (peptide < 8) & (number >= lo) & (number < high)
        best = jnp.maximum(best, jnp.where(inside, scores, -jnp.inf))
        total = total + jnp.where(inside, scores, 0.0)

    for reach in (4, 2, 1):
        best = jnp.maximum(best, pltpu.roll(best, wide - reach, 1))
        total = total + pltpu.roll(total, wide - reach, 1)
    total = total / length
    spread = lax.broadcasted_iota(jnp.int32, (rows, LANES), 1)
    pick = (spread % 8) * 16
    packed = jnp.zeros((rows, LANES), jnp.float32)
    for n, source in enumerate((best, total)):
        for v in range(wide // LANES):
            place = n * shifts + v * 8
            taken = jnp.take_along_axis(source[:, v * LANES:(v + 1) * LANES], pick, axis=1)
            packed = jnp.where((spread >= place) & (spread < place + 8), taken, packed)
    for q in range(nq):
        send[q, :own] = packed[q * own:(q + 1) * own]

    def result_copy(d):
        return pltpu.make_async_remote_copy(
            src_ref=send.at[lax.rem(query + d, nq)],
            dst_ref=recv.at[d],
            send_sem=query_send.at[d],
            recv_sem=query_recv.at[d],
            device_id={"query": lax.rem(query + d, nq)},
            device_id_type=MESH,
        )

    for d in range(1, nq):
        result_copy(d).start()
    mine = send[query]
    top, mean = mine, mine
    for d in range(1, nq):
        result_copy(d).wait_recv()
        top = jnp.maximum(top, recv[d])
        mean = mean + recv[d]
    place = lax.broadcasted_iota(jnp.int32, top.shape, 1)
    out_ref[...] = jnp.where(place < shifts, top, mean)[:own, :2 * shifts]
    for h in range(PARTS):
        for d in range(1, nb):
            theo_copy(d, h).wait_send()
    for d in range(1, nq):
        result_copy(d).wait_send()


def local(spectra, theo, offsets, win_lo, win_len):
    nb, nq = lax.axis_size("band"), lax.axis_size("query")
    rows, bins = spectra.shape
    peps = theo.shape[1]
    shifts = offsets.shape[0]
    own = rows // nq
    slots = (own + 7) // 8 * 8
    chunks = nb * peps // 8
    result = jax.ShapeDtypeStruct((own, 2 * shifts), jnp.float32)
    vmem = pl.BlockSpec(memory_space=pltpu.VMEM)
    both = pl.pallas_call(
        functools.partial(kernel, nb, nq),
        out_shape=result,
        in_specs=[
            pl.BlockSpec(memory_space=pltpu.HBM),
        ] * 5,
        out_specs=vmem,
        scratch_shapes=[
            pltpu.VMEM((rows, bins + 2 * LANES), jnp.bfloat16),
            pltpu.VMEM((rows, bins), jnp.bfloat16),
            pltpu.VMEM((nb, peps, bins + LANES), jnp.bfloat16),
            pltpu.VMEM((chunks, bins // LANES + 2, 16, LANES), jnp.bfloat16),
            pltpu.VMEM((2, BLOCK, BLOCK), jnp.bfloat16),
            pltpu.VMEM((nq, slots, LANES), jnp.float32),
            pltpu.VMEM((nq, slots, LANES), jnp.float32),
            pltpu.SMEM((shifts,), jnp.int32),
            pltpu.VMEM((rows,), jnp.int32),
            pltpu.VMEM((rows,), jnp.int32),
            pltpu.SemaphoreType.DMA((3,)),
            pltpu.SemaphoreType.DMA((bins // (BLOCK * BOX_BLOCKS),)),
            pltpu.SemaphoreType.DMA,
            pltpu.SemaphoreType.DMA((nb, PARTS)),
            pltpu.SemaphoreType.DMA((nb, PARTS)),
            pltpu.SemaphoreType.DMA((nq,)),
            pltpu.SemaphoreType.DMA((nq,)),
        ],
        compiler_params=pltpu.CompilerParams(
            collective_id=0, has_side_effects=True, vmem_limit_bytes=64 * 2**20
        ),
        name="shifted_scores",
    )(spectra, theo, offsets, win_lo, win_len)
    return both[:, :shifts], both[:, shifts:]


def solution(mesh):
    placed = (P("band", None), P("query", "band", None), P(), P("band"), P("band"))
    return jax.shard_map(
        local,
        mesh=mesh,
        in_specs=placed,
        out_specs=(P(("band", "query"), None), P(("band", "query"), None)),
        check_vma=False,
    )
```

```python
import functools

import jax
import jax.numpy as jnp
from jax import lax
from jax.experimental import pallas as pl
from jax.experimental.pallas import tpu as pltpu
from jax.sharding import PartitionSpec as P

BG_HALF = 75
SHIFT_MAX = 128
LANES = 128
BLOCK = 256
BOX_BLOCKS = 16
STEP = 4096
PARTS = 2
MESH = pl.DeviceIdType.MESH


def box_tables():
    row = lax.broadcasted_iota(jnp.int32, (BLOCK, BLOCK), 0)
    target = lax.broadcasted_iota(jnp.int32, (BLOCK, BLOCK), 1)
    gap = row - target
    middle = (jnp.abs(gap) <= BG_HALF) & (gap != 0)
    side_gap = jnp.where(row < LANES, row - LANES, row + LANES) - target
    side = jnp.abs(side_gap) <= BG_HALF
    return middle.astype(jnp.float32).astype(jnp.bfloat16), side.astype(jnp.float32).astype(jnp.bfloat16)


def column(values, rows):
    row = lax.broadcasted_iota(jnp.int32, (rows, rows), 0)
    lane = lax.broadcasted_iota(jnp.int32, (rows, rows), 1)
    spread = jnp.broadcast_to(values.astype(jnp.float32).reshape(1, rows), (rows, rows))
    return jnp.sum(jnp.where(row == lane, spread, 0.0), axis=1, keepdims=True)


def kernel(
    nb, nq,
    spectra_ref, theo_ref, offsets_hbm, lo_hbm, len_hbm,
    out_ref,
    spec, corr, gathered, pairs, tables, send, recv,
    offsets_ref, lo_ref, len_ref, small_sem, spec_sem, own_sem, band_send, band_recv, query_send, query_recv,
):
    rows, bins = spectra_ref.shape
    peps = theo_ref.shape[1]
    shifts = offsets_hbm.shape[0]
    own = rows // nq
    blocks = bins // LANES
    per_chunk = 8 // peps
    chunks = nb * peps // 8
    width = BLOCK * BOX_BLOCKS
    box_steps = bins // width
    band = lax.axis_index("band")
    query = lax.axis_index("query")

    barrier = pltpu.get_barrier_semaphore()
    for d in range(1, nb):
        pl.semaphore_signal(barrier, inc=1, device_id={"band": lax.rem(band + d, nb)}, device_id_type=MESH)
    for d in range(1, nq):
        pl.semaphore_signal(barrier, inc=1, device_id={"query": lax.rem(query + d, nq)}, device_id_type=MESH)

    def spec_copy(i):
        start = pl.multiple_of(i * width, width)
        return pltpu.make_async_copy(
            spectra_ref.at[:, pl.ds(start, width)],
            spec.at[:, pl.ds(pl.multiple_of(start + LANES, LANES), width)],
            spec_sem.at[i],
        )

    for i in range(box_steps):
        spec_copy(i).start()
    own_copy = pltpu.make_async_copy(theo_ref.at[0], gathered.at[0, :, pl.ds(0, bins)], own_sem)
    own_copy.start()
    small = [
        pltpu.make_async_copy(source, target, small_sem.at[i])
        for i, (source, target) in enumerate(
            [(offsets_hbm, offsets_ref), (lo_hbm, lo_ref), (len_hbm, len_ref)]
        )
    ]
    for copy in small:
        copy.start()

    pl.semaphore_wait(barrier, nb - 1 + nq - 1)

    part = bins // PARTS

    def theo_copy(d, h):
        return pltpu.make_async_remote_copy(
            src_ref=theo_ref.at[0, :, pl.ds(h * part, part)],
            dst_ref=gathered.at[d, :, pl.ds(h * part, part)],
            send_sem=band_send.at[d, h],
            recv_sem=band_recv.at[d, h],
            device_id={"band": lax.rem(band + d, nb)},
            device_id_type=MESH,
        )

    for h in range(PARTS):
        for d in range(1, nb):
            theo_copy(d, h).start()

    spec[:, :LANES] = jnp.zeros((rows, LANES), spec.dtype)
    spec[:, LANES + bins:] = jnp.zeros((rows, LANES), spec.dtype)
    tables[0], tables[1] = box_tables()
    send[...] = jnp.zeros_like(send)
    gathered[:, :, bins:] = jnp.zeros((nb, peps, LANES), gathered.dtype)
    for c in range(chunks):
        pairs[c, blocks + 1] = jnp.zeros((16, LANES), pairs.dtype)
    for copy in small:
        copy.wait()
    lo = column(lo_ref[...], rows)
    length = column(len_ref[...], rows)
    high = lo + length

    spec_copy(0).wait()

    @pl.loop(0, box_steps)
    def _(i):
        @pl.when(i + 1 < box_steps)
        def _():
            spec_copy(i + 1).wait()

        start = pl.multiple_of(i * width, width)
        middles, sides = [], []
        for j in range(BOX_BLOCKS):
            at = start + j * BLOCK
            before = spec[:, pl.ds(pl.multiple_of(at, LANES), LANES)]
            middles.append(spec[:, pl.ds(pl.multiple_of(at + LANES, LANES), BLOCK)])
            after = spec[:, pl.ds(pl.multiple_of(at + LANES + BLOCK, LANES), LANES)]
            sides.append(jnp.concatenate([before, after], axis=1))
        box = jnp.dot(jnp.concatenate(middles, axis=0), tables[0], preferred_element_type=jnp.float32)
        box += jnp.dot(jnp.concatenate(sides, axis=0), tables[1], preferred_element_type=jnp.float32)
        for j in range(BOX_BLOCKS):
            level = box[j * rows:(j + 1) * rows] * (1.0 / (2.0 * BG_HALF))
            fixed = middles[j].astype(jnp.float32) - level
            corr[:, pl.ds(pl.multiple_of(start + j * BLOCK, BLOCK), BLOCK)] = fixed.astype(jnp.bfloat16)

    own_copy.wait()
    lane = lax.broadcasted_iota(jnp.int32, (16, LANES), 1).astype(jnp.float32).astype(jnp.bfloat16)
    ahead = [SHIFT_MAX - offsets_ref[k] for k in range(shifts)]
    skip = [a // LANES for a in ahead]
    rest = [a % LANES for a in ahead]
    turn = [(LANES - r) % LANES for r in rest]
    edge = [jnp.full((16, LANES), r.astype(jnp.float32)).astype(jnp.bfloat16) for r in rest]
    per_step = STEP // LANES
    wide = shifts * 16

    def read_blocks(c, first):
        at = pl.ds(pl.multiple_of(first * LANES, LANES), 9 * LANES)
        rows_of = []
        for j in range(per_chunk):
            slot = lax.rem(band - (c * per_chunk + j) + nb, nb)
            rows_of.append(gathered[slot, :, at].astype(jnp.float32))
        whole = jnp.concatenate(rows_of, axis=0)
        return [whole[:, t * LANES:(t + 1) * LANES] for t in range(9)]

    def pair(c, g):
        found = read_blocks(c, g * 8)
        for t in range(8):
            pairs[c, g * 8 + t + 1] = jnp.concatenate(found[t:t + 2], axis=0).astype(jnp.bfloat16)

    def step(c, i, acc):
        first = i * per_step
        columns, evens, odds = [], [], []
        for j in range(0, per_step, 2):
            parts = []
            for k in range(shifts):
                near = pairs[c, first + j + skip[k]]
                far = pairs[c, first + j + skip[k] + 1]
                parts.append(pltpu.roll(jnp.where(lane < edge[k], far, near), turn[k], 1))
            columns.append(jnp.concatenate(parts, axis=0))
            at = (first + j) * LANES
            evens.append(corr[:, pl.ds(pl.multiple_of(at, LANES), LANES)])
            odds.append(corr[:, pl.ds(pl.multiple_of(at + LANES, LANES), LANES)])
        shifted = jnp.concatenate(columns, axis=1)
        piece = jnp.concatenate(
            [jnp.concatenate(evens, axis=1), jnp.concatenate(odds, axis=1)], axis=0
        )
        return acc + lax.dot_general(
            piece, shifted, (((1,), (1,)), ((), ())), preferred_element_type=jnp.float32
        )

    sums = [jnp.zeros((2 * rows, wide), jnp.float32)] * chunks
    group_from = step_from = 0
    for h in range(PARTS):
        for d in range(1, nb):
            theo_copy(d, h).wait_recv()
        if h < PARTS - 1:
            group_to = ((h + 1) * part // LANES - 1) // 8
            step_to = (group_to * 8 - per_step - 1) // per_step + 1
        else:
            group_to, step_to = blocks // 8, bins // STEP
        for c in range(chunks):
            if h == 0:
                start = read_blocks(c, 0)[0]
                pairs[c, 0] = jnp.concatenate([jnp.zeros_like(start), start], axis=0).astype(jnp.bfloat16)
            pl.loop(group_from, group_to, unroll=True)(functools.partial(pair, c))
            sums[c] = lax.fori_loop(step_from, step_to, functools.partial(step, c), sums[c])
        group_from, step_from = group_to, step_to

    spread = lax.broadcasted_iota(jnp.int32, (rows, wide), 1)
    peptide = spread % 16
    best = jnp.full((rows, wide), -jnp.inf, jnp.float32)
    total = jnp.zeros((rows, wide), jnp.float32)
    for c in range(chunks):
        scores = sums[c][:rows] + pltpu.roll(sums[c][rows:], wide - 8, 1)
        number = (peptide + (query * (chunks * 8) + c * 8)).astype(jnp.float32)
        inside = (peptide < 8) & (number >= lo) & (number < high)
        best = jnp.maximum(best, jnp.where(inside, scores, -jnp.inf))
        total = total + jnp.where(inside, scores, 0.0)

    for reach in (4, 2, 1):
        best = jnp.maximum(best, pltpu.roll(best, wide - reach, 1))
        total = total + pltpu.roll(total, wide - reach, 1)
    total = total / length
    spread = lax.broadcasted_iota(jnp.int32, (rows, LANES), 1)
    pick = (spread % 8) * 16
    packed = jnp.zeros((rows, LANES), jnp.float32)
    for n, source in enumerate((best, total)):
        for v in range(wide // LANES):
            place = n * shifts + v * 8
            taken = jnp.take_along_axis(source[:, v * LANES:(v + 1) * LANES], pick, axis=1)
            packed = jnp.where((spread >= place) & (spread < place + 8), taken, packed)
    for q in range(nq):
        send[q, :own] = packed[q * own:(q + 1) * own]

    def result_copy(d):
        return pltpu.make_async_remote_copy(
            src_ref=send.at[lax.rem(query + d, nq)],
            dst_ref=recv.at[d],
            send_sem=query_send.at[d],
            recv_sem=query_recv.at[d],
            device_id={"query": lax.rem(query + d, nq)},
            device_id_type=MESH,
        )

    for d in range(1, nq):
        result_copy(d).start()
    mine = send[query]
    top, mean = mine, mine
    for d in range(1, nq):
        result_copy(d).wait_recv()
        top = jnp.maximum(top, recv[d])
        mean = mean + recv[d]
    out_ref[0] = top[:own, :shifts]
    out_ref[1] = pltpu.roll(mean, LANES - shifts, 1)[:own, :shifts]
    for h in range(PARTS):
        for d in range(1, nb):
            theo_copy(d, h).wait_send()
    for d in range(1, nq):
        result_copy(d).wait_send()


def local(spectra, theo, offsets, win_lo, win_len):
    nb, nq = lax.axis_size("band"), lax.axis_size("query")
    rows, bins = spectra.shape
    peps = theo.shape[1]
    shifts = offsets.shape[0]
    own = rows // nq
    slots = (own + 7) // 8 * 8
    chunks = nb * peps // 8
    result = jax.ShapeDtypeStruct((2, own, shifts), jnp.float32)
    vmem = pl.BlockSpec(memory_space=pltpu.VMEM)
    both = pl.pallas_call(
        functools.partial(kernel, nb, nq),
        out_shape=result,
        in_specs=[
            pl.BlockSpec(memory_space=pltpu.HBM),
        ] * 5,
        out_specs=vmem,
        scratch_shapes=[
            pltpu.VMEM((rows, bins + 2 * LANES), jnp.bfloat16),
            pltpu.VMEM((rows, bins), jnp.bfloat16),
            pltpu.VMEM((nb, peps, bins + LANES), jnp.bfloat16),
            pltpu.VMEM((chunks, bins // LANES + 2, 16, LANES), jnp.bfloat16),
            pltpu.VMEM((2, BLOCK, BLOCK), jnp.bfloat16),
            pltpu.VMEM((nq, slots, LANES), jnp.float32),
            pltpu.VMEM((nq, slots, LANES), jnp.float32),
            pltpu.SMEM((shifts,), jnp.int32),
            pltpu.VMEM((rows,), jnp.int32),
            pltpu.VMEM((rows,), jnp.int32),
            pltpu.SemaphoreType.DMA((3,)),
            pltpu.SemaphoreType.DMA((bins // (BLOCK * BOX_BLOCKS),)),
            pltpu.SemaphoreType.DMA,
            pltpu.SemaphoreType.DMA((nb, PARTS)),
            pltpu.SemaphoreType.DMA((nb, PARTS)),
            pltpu.SemaphoreType.DMA((nq,)),
            pltpu.SemaphoreType.DMA((nq,)),
        ],
        compiler_params=pltpu.CompilerParams(
            collective_id=0, has_side_effects=True, vmem_limit_bytes=64 * 2**20
        ),
        name="shifted_scores",
    )(spectra, theo, offsets, win_lo, win_len)
    return both[0], both[1]


def solution(mesh):
    placed = (P("band", None), P("query", "band", None), P(), P("band"), P("band"))
    return jax.shard_map(
        local,
        mesh=mesh,
        in_specs=placed,
        out_specs=(P(("band", "query"), None), P(("band", "query"), None)),
        check_vma=False,
    )
```

```python
import functools

import jax
import jax.numpy as jnp
from jax import lax
from jax.experimental import pallas as pl
from jax.experimental.pallas import tpu as pltpu
from jax.sharding import PartitionSpec as P

BG_HALF = 75
SHIFT_MAX = 128
LANES = 128
BLOCK = 256
BOX_BLOCKS = 16
STEP = 4096
PARTS = 2
MESH = pl.DeviceIdType.MESH


def box_tables():
    row = lax.broadcasted_iota(jnp.int32, (BLOCK, BLOCK), 0)
    target = lax.broadcasted_iota(jnp.int32, (BLOCK, BLOCK), 1)
    gap = row - target
    middle = (jnp.abs(gap) <= BG_HALF) & (gap != 0)
    side_gap = jnp.where(row < LANES, row - LANES, row + LANES) - target
    side = jnp.abs(side_gap) <= BG_HALF
    return middle.astype(jnp.float32).astype(jnp.bfloat16), side.astype(jnp.float32).astype(jnp.bfloat16)


def column(values, rows):
    row = lax.broadcasted_iota(jnp.int32, (rows, rows), 0)
    lane = lax.broadcasted_iota(jnp.int32, (rows, rows), 1)
    spread = jnp.broadcast_to(values.astype(jnp.float32).reshape(1, rows), (rows, rows))
    return jnp.sum(jnp.where(row == lane, spread, 0.0), axis=1, keepdims=True)


def kernel(
    nb, nq,
    spectra_ref, theo_ref, offsets_hbm, lo_hbm, len_hbm,
    out_ref,
    spec, corr, gathered, pairs, tables, send, recv,
    offsets_ref, lo_ref, len_ref, small_sem, spec_sem, own_sem, band_send, band_recv, query_send, query_recv,
):
    rows, bins = spectra_ref.shape
    peps = theo_ref.shape[1]
    shifts = offsets_hbm.shape[0]
    own = rows // nq
    blocks = bins // LANES
    per_chunk = 8 // peps
    chunks = nb * peps // 8
    width = BLOCK * BOX_BLOCKS
    box_steps = bins // width
    band = lax.axis_index("band")
    query = lax.axis_index("query")

    barrier = pltpu.get_barrier_semaphore()
    for d in range(1, nb):
        pl.semaphore_signal(barrier, inc=1, device_id={"band": lax.rem(band + d, nb)}, device_id_type=MESH)
    for d in range(1, nq):
        pl.semaphore_signal(barrier, inc=1, device_id={"query": lax.rem(query + d, nq)}, device_id_type=MESH)

    def spec_copy(i):
        start = pl.multiple_of(i * width, width)
        return pltpu.make_async_copy(
            spectra_ref.at[:, pl.ds(start, width)],
            spec.at[:, pl.ds(pl.multiple_of(start + LANES, LANES), width)],
            spec_sem.at[i],
        )

    for i in range(box_steps):
        spec_copy(i).start()
    own_copy = pltpu.make_async_copy(theo_ref.at[0], gathered.at[0, :, pl.ds(0, bins)], own_sem)
    own_copy.start()
    small = [
        pltpu.make_async_copy(source, target, small_sem.at[i])
        for i, (source, target) in enumerate(
            [(offsets_hbm, offsets_ref), (lo_hbm, lo_ref), (len_hbm, len_ref)]
        )
    ]
    for copy in small:
        copy.start()

    pl.semaphore_wait(barrier, nb - 1 + nq - 1)

    part = bins // PARTS

    def theo_copy(d, h):
        return pltpu.make_async_remote_copy(
            src_ref=theo_ref.at[0, :, pl.ds(h * part, part)],
            dst_ref=gathered.at[d, :, pl.ds(h * part, part)],
            send_sem=band_send.at[d, h],
            recv_sem=band_recv.at[d, h],
            device_id={"band": lax.rem(band + d, nb)},
            device_id_type=MESH,
        )

    for h in range(PARTS):
        for d in sorted(range(1, nb), key=lambda d: abs(d - nb // 2)):
            theo_copy(d, h).start()

    spec[:, :LANES] = jnp.zeros((rows, LANES), spec.dtype)
    spec[:, LANES + bins:] = jnp.zeros((rows, LANES), spec.dtype)
    tables[0], tables[1] = box_tables()
    send[...] = jnp.zeros_like(send)
    gathered[:, :, bins:] = jnp.zeros((nb, peps, LANES), gathered.dtype)
    for c in range(chunks):
        pairs[c, blocks + 1] = jnp.zeros((16, LANES), pairs.dtype)
    for copy in small:
        copy.wait()
    lo = column(lo_ref[...], rows)
    length = column(len_ref[...], rows)
    high = lo + length

    spec_copy(0).wait()

    @pl.loop(0, box_steps)
    def _(i):
        @pl.when(i + 1 < box_steps)
        def _():
            spec_copy(i + 1).wait()

        start = pl.multiple_of(i * width, width)
        middles, sides = [], []
        for j in range(BOX_BLOCKS):
            at = start + j * BLOCK
            before = spec[:, pl.ds(pl.multiple_of(at, LANES), LANES)]
            middles.append(spec[:, pl.ds(pl.multiple_of(at + LANES, LANES), BLOCK)])
            after = spec[:, pl.ds(pl.multiple_of(at + LANES + BLOCK, LANES), LANES)]
            sides.append(jnp.concatenate([before, after], axis=1))
        box = jnp.dot(jnp.concatenate(middles, axis=0), tables[0], preferred_element_type=jnp.float32)
        box += jnp.dot(jnp.concatenate(sides, axis=0), tables[1], preferred_element_type=jnp.float32)
        for j in range(BOX_BLOCKS):
            level = box[j * rows:(j + 1) * rows] * (1.0 / (2.0 * BG_HALF))
            fixed = middles[j].astype(jnp.float32) - level
            corr[:, pl.ds(pl.multiple_of(start + j * BLOCK, BLOCK), BLOCK)] = fixed.astype(jnp.bfloat16)

    own_copy.wait()
    lane = lax.broadcasted_iota(jnp.int32, (16, LANES), 1).astype(jnp.float32).astype(jnp.bfloat16)
    ahead = [SHIFT_MAX - offsets_ref[k] for k in range(shifts)]
    skip = [a // LANES for a in ahead]
    rest = [a % LANES for a in ahead]
    turn = [(LANES - r) % LANES for r in rest]
    edge = [jnp.full((16, LANES), r.astype(jnp.float32)).astype(jnp.bfloat16) for r in rest]
    per_step = STEP // LANES
    wide = shifts * 16

    def read_blocks(c, first):
        at = pl.ds(pl.multiple_of(first * LANES, LANES), 9 * LANES)
        rows_of = []
        for j in range(per_chunk):
            slot = lax.rem(band - (c * per_chunk + j) + nb, nb)
            rows_of.append(gathered[slot, :, at].astype(jnp.float32))
        whole = jnp.concatenate(rows_of, axis=0)
        return [whole[:, t * LANES:(t + 1) * LANES] for t in range(9)]

    def pair(c, g):
        found = read_blocks(c, g * 8)
        for t in range(8):
            pairs[c, g * 8 + t + 1] = jnp.concatenate(found[t:t + 2], axis=0).astype(jnp.bfloat16)

    def step(c, i, acc):
        first = i * per_step
        columns, evens, odds = [], [], []
        for j in range(0, per_step, 2):
            parts = []
            for k in range(shifts):
                near = pairs[c, first + j + skip[k]]
                far = pairs[c, first + j + skip[k] + 1]
                parts.append(pltpu.roll(jnp.where(lane < edge[k], far, near), turn[k], 1))
            columns.append(jnp.concatenate(parts, axis=0))
            at = (first + j) * LANES
            evens.append(corr[:, pl.ds(pl.multiple_of(at, LANES), LANES)])
            odds.append(corr[:, pl.ds(pl.multiple_of(at + LANES, LANES), LANES)])
        shifted = jnp.concatenate(columns, axis=1)
        piece = jnp.concatenate(
            [jnp.concatenate(evens, axis=1), jnp.concatenate(odds, axis=1)], axis=0
        )
        return acc + lax.dot_general(
            piece, shifted, (((1,), (1,)), ((), ())), preferred_element_type=jnp.float32
        )

    sums = [jnp.zeros((2 * rows, wide), jnp.float32)] * chunks
    group_from = step_from = 0
    for h in range(PARTS):
        for d in range(1, nb):
            theo_copy(d, h).wait_recv()
        if h < PARTS - 1:
            group_to = ((h + 1) * part // LANES - 1) // 8
            step_to = (group_to * 8 - per_step - 1) // per_step + 1
        else:
            group_to, step_to = blocks // 8, bins // STEP
        for c in range(chunks):
            if h == 0:
                start = read_blocks(c, 0)[0]
                pairs[c, 0] = jnp.concatenate([jnp.zeros_like(start), start], axis=0).astype(jnp.bfloat16)
            pl.loop(group_from, group_to, unroll=True)(functools.partial(pair, c))
            sums[c] = lax.fori_loop(step_from, step_to, functools.partial(step, c), sums[c])
        group_from, step_from = group_to, step_to

    spread = lax.broadcasted_iota(jnp.int32, (rows, wide), 1)
    peptide = spread % 16
    best = jnp.full((rows, wide), -jnp.inf, jnp.float32)
    total = jnp.zeros((rows, wide), jnp.float32)
    for c in range(chunks):
        scores = sums[c][:rows] + pltpu.roll(sums[c][rows:], wide - 8, 1)
        number = (peptide + (query * (chunks * 8) + c * 8)).astype(jnp.float32)
        inside = (peptide < 8) & (number >= lo) & (number < high)
        best = jnp.maximum(best, jnp.where(inside, scores, -jnp.inf))
        total = total + jnp.where(inside, scores, 0.0)

    for reach in (4, 2, 1):
        best = jnp.maximum(best, pltpu.roll(best, wide - reach, 1))
        total = total + pltpu.roll(total, wide - reach, 1)
    total = total / length
    spread = lax.broadcasted_iota(jnp.int32, (rows, LANES), 1)
    pick = (spread % 8) * 16
    packed = jnp.zeros((rows, LANES), jnp.float32)
    for n, source in enumerate((best, total)):
        for v in range(wide // LANES):
            place = n * shifts + v * 8
            taken = jnp.take_along_axis(source[:, v * LANES:(v + 1) * LANES], pick, axis=1)
            packed = jnp.where((spread >= place) & (spread < place + 8), taken, packed)
    for q in range(nq):
        send[q, :own] = packed[q * own:(q + 1) * own]

    def result_copy(d):
        return pltpu.make_async_remote_copy(
            src_ref=send.at[lax.rem(query + d, nq)],
            dst_ref=recv.at[d],
            send_sem=query_send.at[d],
            recv_sem=query_recv.at[d],
            device_id={"query": lax.rem(query + d, nq)},
            device_id_type=MESH,
        )

    for d in range(1, nq):
        result_copy(d).start()
    mine = send[query]
    top, mean = mine, mine
    for d in range(1, nq):
        result_copy(d).wait_recv()
        top = jnp.maximum(top, recv[d])
        mean = mean + recv[d]
    out_ref[0] = top[:own, :shifts]
    out_ref[1] = pltpu.roll(mean, LANES - shifts, 1)[:own, :shifts]
    for h in range(PARTS):
        for d in range(1, nb):
            theo_copy(d, h).wait_send()
    for d in range(1, nq):
        result_copy(d).wait_send()


def local(spectra, theo, offsets, win_lo, win_len):
    nb, nq = lax.axis_size("band"), lax.axis_size("query")
    rows, bins = spectra.shape
    peps = theo.shape[1]
    shifts = offsets.shape[0]
    own = rows // nq
    slots = (own + 7) // 8 * 8
    chunks = nb * peps // 8
    result = jax.ShapeDtypeStruct((2, own, shifts), jnp.float32)
    vmem = pl.BlockSpec(memory_space=pltpu.VMEM)
    both = pl.pallas_call(
        functools.partial(kernel, nb, nq),
        out_shape=result,
        in_specs=[
            pl.BlockSpec(memory_space=pltpu.HBM),
        ] * 5,
        out_specs=vmem,
        scratch_shapes=[
            pltpu.VMEM((rows, bins + 2 * LANES), jnp.bfloat16),
            pltpu.VMEM((rows, bins), jnp.bfloat16),
            pltpu.VMEM((nb, peps, bins + LANES), jnp.bfloat16),
            pltpu.VMEM((chunks, bins // LANES + 2, 16, LANES), jnp.bfloat16),
            pltpu.VMEM((2, BLOCK, BLOCK), jnp.bfloat16),
            pltpu.VMEM((nq, slots, LANES), jnp.float32),
            pltpu.VMEM((nq, slots, LANES), jnp.float32),
            pltpu.SMEM((shifts,), jnp.int32),
            pltpu.VMEM((rows,), jnp.int32),
            pltpu.VMEM((rows,), jnp.int32),
            pltpu.SemaphoreType.DMA((3,)),
            pltpu.SemaphoreType.DMA((bins // (BLOCK * BOX_BLOCKS),)),
            pltpu.SemaphoreType.DMA,
            pltpu.SemaphoreType.DMA((nb, PARTS)),
            pltpu.SemaphoreType.DMA((nb, PARTS)),
            pltpu.SemaphoreType.DMA((nq,)),
            pltpu.SemaphoreType.DMA((nq,)),
        ],
        compiler_params=pltpu.CompilerParams(
            collective_id=0, has_side_effects=True, vmem_limit_bytes=64 * 2**20
        ),
        name="shifted_scores",
    )(spectra, theo, offsets, win_lo, win_len)
    return both[0], both[1]


def solution(mesh):
    placed = (P("band", None), P("query", "band", None), P(), P("band"), P("band"))
    return jax.shard_map(
        local,
        mesh=mesh,
        in_specs=placed,
        out_specs=(P(("band", "query"), None), P(("band", "query"), None)),
        check_vma=False,
    )
```
